32 devices in a mesh: hi: 4 (over z), mid: 4 (over x, core), lo: 2 (over y).
Axes of the slice: x: 2, y: 2, z: 4, core: 2. Of those that a mesh axis runs over, the one named last changes fastest.
Arguments:
- amplitudes: bfloat16 [1024, 16384], P('lo', ('hi', 'mid')), may hold values from -6 to 6
- hop_blocks: bfloat16 [4, 512, 512], replicated, may hold values from -1 to 2, as said below
- coupling_seed: int32 [14], replicated, may hold values from 1 to 7
Outputs:
- new_state: bfloat16 [1024, 16384], P('lo', ('hi', 'mid'))
The draws below stay inside these ranges and needn't reach their ends.
Inputs may be any that keep to these rules, and one draw needn't show every extreme that they name: hop_blocks[k, a, b] is zero where a and b differ in their number of set bits.
All inputs are finite; a program needn't handle non-finite values.
Results may differ from the reference program's by a relative error of at most 0.0064.
Values may be sent and summed in bfloat16 or wider, within the bound.
A program may use at most 64 MiB of HBM per device.

```python
import math
import jax
import jax.numpy as jnp
from jax import lax

BLOCK = 512
SITES = 14
NU = 16384
ND = 1024


def draw_hop_blocks(key, part):
    noise = jnp.clip(jax.random.normal(key, (4, BLOCK, BLOCK), jnp.float32), -4.0, 4.0)
    config_ids = jnp.arange(BLOCK, dtype=jnp.int32)
    counted = jnp.zeros((BLOCK,), jnp.int32)
    for bit_pos in range(16):
        counted = counted + (config_ids >> bit_pos & 1)
    same_count = (counted[:, None] == counted[None, :]).astype(jnp.float32)
    identity = jnp.eye(BLOCK, dtype=jnp.float32)
    return (identity[None, :, :] + 0.5 * noise * same_count[None, :, :] / math.sqrt(BLOCK)).astype(jnp.bfloat16)


def with_ends(entries, stream_key, least, largest):
    longest = entries.shape.index(max(entries.shape))
    spots = []
    for shift in (0, 1):
        where = [jax.random.randint(jax.random.fold_in(stream_key, axis), (), 0, length) for axis, length in enumerate(entries.shape)]
        where[longest] = (where[longest] + shift) % entries.shape[longest]
        spots.append(tuple(where))
    return entries.at[spots[0]].set(least).at[spots[1]].set(largest)


def levels(stream_key, dims, split, least, high):
    loudness = 1.0
    for axis_at, blocks in split:
        draws = jax.random.uniform(jax.random.fold_in(jax.random.fold_in(stream_key, 6), axis_at), (blocks,), jnp.float32, least / len(split), high / len(split))
        loudness = loudness * jnp.repeat(jnp.exp(draws), dims[axis_at] // blocks).reshape((-1,) + (1,) * (len(dims) - 1 - axis_at))
    return loudness


def bell_draw(stream_key, dims, width, most, pieces=(), held_as=jnp.bfloat16):
    drawn = width * jax.random.normal(stream_key, dims, jnp.float32)
    if pieces:
        drawn = drawn * levels(stream_key, dims, pieces, -0.22, 0.18)
    return jnp.clip(drawn, -most, most).astype(held_as)


def setup_inputs(seed: int = 0) -> dict:
    key_of = jax.random.split(jax.random.key(seed), 4)
    amplitudes = bell_draw(key_of[0], (ND, NU), 1.0, 6.0, ((0, 2), (1, 16)))
    hop_blocks = draw_hop_blocks(jax.random.fold_in(key_of[3], 71), 0)
    coupling_seed = with_ends(jax.random.randint(key_of[2], (SITES,), 1, 8), jax.random.fold_in(key_of[2], 1), 1, 7).astype(jnp.int32)
    return {"amplitudes": amplitudes, "hop_blocks": hop_blocks, "coupling_seed": coupling_seed}


COUPLING = 0.06


def occupancy(indices):
    site_ids = jnp.arange(SITES, dtype=jnp.int32)
    return ((indices[:, None] >> site_ids[None, :]) & 1).astype(jnp.float32)


def diagonal_factor(up_index, down_index, coupling_seed):
    up_occupied = occupancy(up_index)
    down_occupied = occupancy(down_index)
    strength = COUPLING * coupling_seed.astype(jnp.float32)
    energy = jnp.dot(up_occupied * strength[None, :], down_occupied.T, precision=lax.Precision.HIGHEST)
    return jnp.exp(-energy)


def reference(amplitudes, hop_blocks, coupling_seed):
    matrices = hop_blocks.astype(jnp.float32)
    row_block = 64
    col_block = 128
    up_index = jnp.arange(NU, dtype=jnp.int32)

    def up_section(packed):
        states, first_row = packed
        values = states.astype(jnp.float32).reshape(row_block, NU // BLOCK, BLOCK)
        first_pass = jnp.einsum("dav,wv->daw", values, matrices[0]).astype(jnp.bfloat16)
        spread = first_pass.astype(jnp.float32).reshape(row_block, BLOCK, NU // BLOCK)
        second_pass = jnp.einsum("gh,dhl->dgl", matrices[1], spread).reshape(row_block, NU)
        down_index = first_row + jnp.arange(row_block, dtype=jnp.int32)
        factor = diagonal_factor(up_index, down_index, coupling_seed).T
        return (second_pass * factor).astype(jnp.bfloat16)

    starts = jnp.arange(ND // row_block, dtype=jnp.int32) * row_block
    mixed_pass = lax.map(up_section, (amplitudes.reshape(ND // row_block, row_block, NU), starts))
    mixed_pass = mixed_pass.reshape(ND, NU)
    columns = mixed_pass.reshape(ND, NU // col_block, col_block).transpose(1, 0, 2)

    def down_section(states):
        values = states.astype(jnp.float32).reshape(ND // BLOCK, BLOCK, col_block)
        third_pass = jnp.einsum("ed,adc->aec", matrices[2], values).astype(jnp.bfloat16)
        spread = third_pass.astype(jnp.float32).reshape(BLOCK, ND // BLOCK, col_block)
        fourth_pass = jnp.einsum("gh,hrc->grc", matrices[3], spread)
        return fourth_pass.reshape(ND, col_block).astype(jnp.bfloat16)

    result = lax.map(down_section, columns)
    return result.transpose(1, 0, 2).reshape(ND, NU)
```

```python
import functools
import math

import jax
import jax.numpy as jnp
from jax import lax
from jax.experimental import pallas as pl
from jax.experimental.pallas import tpu as pltpu
from jax.sharding import PartitionSpec as P

SITES = 14
COUPLING = 0.06
AXES = ("hi", "mid", "lo")
F32, BF16 = jnp.float32, jnp.bfloat16


def occupancy(indices):
    site_ids = jnp.arange(SITES, dtype=jnp.int32)
    return (indices[:, None] >> site_ids[None, :] & 1).astype(jnp.float32)


def diagonal_factor(up_index, down_index, coupling_seed):
    up_occupied = occupancy(up_index)
    down_occupied = occupancy(down_index)
    strength = COUPLING * coupling_seed.astype(jnp.float32)
    energy = jnp.dot(
        up_occupied * strength[None, :], down_occupied.T, precision=lax.Precision.HIGHEST
    )
    return jnp.exp(-energy)


def by_collectives(amplitudes, hop_blocks, coupling_seed):
    block = hop_blocks.shape[1]
    down_rows, up_cols = amplitudes.shape
    groups = lax.axis_size(("hi", "mid"))
    lo_count = lax.axis_size("lo")
    split_view = amplitudes.reshape(down_rows, up_cols // block, block)
    first_pass = jnp.einsum(
        "dav,wv->awd", split_view, hop_blocks[0], preferred_element_type=jnp.float32
    ).astype(jnp.bfloat16)
    local_top = block // groups
    remainder = up_cols // local_top
    first_pass = first_pass.reshape(local_top, remainder, down_rows)
    moved = lax.all_to_all(first_pass, ("hi", "mid"), split_axis=1, concat_axis=0, tiled=True)
    second_pass = jnp.einsum(
        "gh,hpd->gpd", hop_blocks[1], moved, preferred_element_type=jnp.float32
    )
    span_low = remainder // groups
    up_index = (
        jnp.arange(block, dtype=jnp.int32)[:, None] * remainder
        + lax.axis_index(("hi", "mid")) * span_low
        + jnp.arange(span_low, dtype=jnp.int32)[None, :]
    ).reshape(-1)
    down_index = lax.axis_index("lo") * down_rows + jnp.arange(down_rows, dtype=jnp.int32)
    factor = diagonal_factor(up_index, down_index, coupling_seed).reshape(
        block, span_low, down_rows
    )
    mixed_pass = (second_pass * factor).astype(jnp.bfloat16)
    returned = lax.all_to_all(
        mixed_pass, ("hi", "mid"), split_axis=0, concat_axis=1, tiled=True
    ).reshape(up_cols, down_rows)
    third_pass = jnp.einsum(
        "ud,ed->eu", returned, hop_blocks[2], preferred_element_type=jnp.float32
    ).astype(jnp.bfloat16)
    gathered = lax.all_to_all(
        third_pass.reshape(block // lo_count, lo_count, up_cols),
        "lo",
        split_axis=1,
        concat_axis=0,
        tiled=True,
    )
    fourth_pass = jnp.einsum(
        "gh,hpu->gpu", hop_blocks[3], gathered, preferred_element_type=jnp.float32
    ).astype(jnp.bfloat16)
    result = lax.all_to_all(fourth_pass, "lo", split_axis=0, concat_axis=1, tiled=True).reshape(
        down_rows, up_cols
    )
    return result


def dot_nn(a, b):
    return lax.dot_general(a, b, (((1,), (0,)), ((), ())), preferred_element_type=F32)


def dot_nt(a, b):
    return lax.dot_general(a, b, (((1,), (1,)), ((), ())), preferred_element_type=F32)


def ones_where(shape, condition):
    rows = lax.broadcasted_iota(jnp.int32, shape, 0)
    cols = lax.broadcasted_iota(jnp.int32, shape, 1)
    return jnp.where(condition(rows, cols), 1.0, 0.0).astype(F32).astype(BF16)


def step_kernel(
    counts,
    low,
    amp_hbm,
    hop_hbm,
    seed_ref,
    out_ref,
    amp,
    hop,
    packed,
    moved,
    factor,
    mixed,
    third,
    fourth,
    final,
    in_sem,
    own_sem,
    send_sem,
    recv_sem,
):
    n_hi, n_mid, n_lo = counts
    devices = n_hi * n_mid * n_lo
    groups = n_hi * n_mid
    block = hop.shape[1]
    tops = block // low
    spans = amp.shape[1] // block
    my_hi, my_mid, my_lo = (lax.axis_index(name) for name in AXES)
    me = (my_hi * n_mid + my_mid) * n_lo + my_lo
    my_group = my_hi * n_mid + my_mid

    amp_in = pltpu.make_async_copy(amp_hbm, amp, in_sem.at[4])
    amp_in.start()
    hop_in = [
        pltpu.make_async_copy(hop_hbm.at[k], hop.at[k], in_sem.at[k]) for k in range(4)
    ]
    for copy in hop_in:
        copy.start()

    def peer(k):
        rest = k // n_hi
        hi = lax.rem(my_hi + lax.rem(k, n_hi), n_hi)
        mid = lax.rem(my_mid + lax.rem(rest, n_mid), n_mid)
        lo = lax.rem(my_lo + rest // n_mid, n_lo)
        return hi, mid, lo

    barrier = pltpu.get_barrier_semaphore()

    def greet(k, carry):
        pl.semaphore_signal(
            barrier, inc=1, device_id=peer(k), device_id_type=pl.DeviceIdType.MESH
        )
        return carry

    lax.fori_loop(1, devices, greet, 0)

    sorter = ones_where((block, block), lambda r, c: c == (r % tops) * low + r // tops)
    hop_in[0].wait()
    hop0 = dot_nn(sorter, hop[0]).astype(BF16)
    amp_in.wait()
    for b in range(spans):
        first = dot_nt(hop0, amp[:, b * block : (b + 1) * block]).astype(BF16)
        packed[:, b] = first.reshape(low, tops, first.shape[1])

    pl.semaphore_wait(barrier, devices - 1)

    def out_copy(hi, mid, lo):
        target = (hi * n_mid + mid) * n_lo + lo
        return pltpu.make_async_remote_copy(
            src_ref=packed.at[target],
            dst_ref=moved.at[my_lo, my_group],
            send_sem=send_sem.at[0, target],
            recv_sem=recv_sem.at[0, me],
            device_id=(hi, mid, lo),
            device_id_type=pl.DeviceIdType.MESH,
        )

    def in_copy(hi, mid, lo):
        source = (hi * n_mid + mid) * n_lo + lo
        return pltpu.make_async_remote_copy(
            src_ref=packed.at[source],
            dst_ref=moved.at[lo, hi * n_mid + mid],
            send_sem=send_sem.at[0, source],
            recv_sem=recv_sem.at[0, source],
            device_id=(hi, mid, lo),
            device_id_type=pl.DeviceIdType.MESH,
        )

    def send_out(k, carry):
        out_copy(*peer(k)).start()
        return carry

    lax.fori_loop(1, devices, send_out, 0)
    own_out = pltpu.make_async_copy(
        packed.at[me], moved.at[my_lo, my_group], own_sem.at[0]
    )
    own_out.start()

    for copy in hop_in[1:]:
        copy.wait()
    halves = block // n_lo
    unzip = ones_where((block, block), lambda r, c: c == (r % halves) * n_lo + r // halves)
    hop2 = dot_nn(unzip, hop[2]).astype(BF16)
    rows = lax.broadcasted_iota(jnp.int32, (block, 16), 0) * low + me
    site_r = lax.broadcasted_iota(jnp.int32, (block, 16), 1)
    strength = jnp.zeros((block, 16), F32)
    for i in range(SITES):
        strength = jnp.where(site_r == i, seed_ref[i].astype(F32), strength)
    up_part = (((rows >> site_r) & 1).astype(F32) * strength).astype(BF16)
    cols = lax.broadcasted_iota(jnp.int32, (16, n_lo * block), 1)
    site_c = lax.broadcasted_iota(jnp.int32, (16, n_lo * block), 0)
    down_part = ((cols >> site_c) & 1).astype(F32).astype(BF16)
    for lo in range(n_lo):
        part = dot_nn(up_part, down_part[:, lo * block : (lo + 1) * block])
        factor[lo] = jnp.exp(-COUPLING * part)

    own_out.wait()

    def wait_in(k, carry):
        in_copy(*peer(k)).wait_recv()
        return carry

    lax.fori_loop(1, devices, wait_in, 0)
    for lo in range(n_lo):
        second = dot_nn(hop[1], moved[lo].reshape(block, block))
        mixed[lo] = (second * factor[lo]).astype(BF16)

    def back_copy(hi, mid, lo):
        target = (hi * n_mid + mid) * n_lo + lo
        return pltpu.make_async_remote_copy(
            src_ref=fourth.at[lo, hi * n_mid + mid],
            dst_ref=final.at[:, me],
            send_sem=send_sem.at[1, target],
            recv_sem=recv_sem.at[1, me],
            device_id=(hi, mid, lo),
            device_id_type=pl.DeviceIdType.MESH,
        )

    def home_copy(hi, mid, lo):
        source = (hi * n_mid + mid) * n_lo + lo
        return pltpu.make_async_remote_copy(
            src_ref=fourth.at[lo, hi * n_mid + mid],
            dst_ref=final.at[:, source],
            send_sem=send_sem.at[1, source],
            recv_sem=recv_sem.at[1, source],
            device_id=(hi, mid, lo),
            device_id_type=pl.DeviceIdType.MESH,
        )

    chunk = block // n_hi
    for step in [*range(1, n_hi), 0]:
        hi = lax.rem(my_hi + step, n_hi)
        at = pl.ds(pl.multiple_of(hi * chunk, chunk), chunk)
        for lo in range(n_lo):
            third[lo] = dot_nt(mixed[lo, at, :], hop2).astype(BF16)
        for r in range(n_lo):
            total = sum(
                dot_nt(
                    third[lo, :, r * halves : (r + 1) * halves],
                    hop[3, :, lo * halves : (lo + 1) * halves],
                )
                for lo in range(n_lo)
            ).astype(BF16)
            for lo in range(n_lo):
                piece = total[:, lo * halves : (lo + 1) * halves]
                fourth[
                    lo,
                    pl.ds(hi * n_mid, n_mid),
                    :,
                    :,
                    r * halves : (r + 1) * halves,
                ] = piece.reshape(n_mid, spans, tops, halves)

        def send_back(k, carry):
            mid = lax.rem(my_mid + lax.rem(k, n_mid), n_mid)
            lo = lax.rem(my_lo + k // n_mid, n_lo)
            back_copy(hi, mid, lo).start()
            return carry

        lax.fori_loop(0 if step else 1, n_mid * n_lo, send_back, 0)
    own_back = pltpu.make_async_copy(
        fourth.at[my_lo, my_group], final.at[:, me], own_sem.at[1]
    )
    own_back.start()
    zipper = ones_where((block, block), lambda r, c: r == (c % halves) * n_lo + c // halves)
    own_back.wait()

    def wait_home(k, carry):
        home_copy(*peer(k)).wait_recv()
        return carry

    lax.fori_loop(1, devices, wait_home, 0)
    for b in range(spans):
        turned = dot_nt(zipper, final[b].reshape(block, block)).astype(BF16)
        out_ref[:, b * block : (b + 1) * block] = dot_nn(turned, sorter).astype(BF16)

    def drain(k, carry):
        out_copy(*peer(k)).wait_send()
        back_copy(*peer(k)).wait_send()
        return carry

    lax.fori_loop(1, devices, drain, 0)


def by_kernel(counts, amplitudes, hop_blocks, coupling_seed):
    n_hi, n_mid, n_lo = counts
    groups, devices = n_hi * n_mid, n_hi * n_mid * n_lo
    block = hop_blocks.shape[1]
    down_rows, up_cols = amplitudes.shape
    low = up_cols * groups // block
    tops = block // low
    spans = up_cols // block
    pair = (n_lo, block, block)
    return pl.pallas_call(
        functools.partial(step_kernel, counts, low),
        out_shape=jax.ShapeDtypeStruct((down_rows, up_cols), BF16),
        in_specs=[
            pl.BlockSpec(memory_space=pl.ANY),
            pl.BlockSpec(memory_space=pl.ANY),
            pl.BlockSpec(memory_space=pltpu.SMEM),
        ],
        out_specs=pl.BlockSpec(memory_space=pltpu.VMEM),
        scratch_shapes=[
            pltpu.VMEM((down_rows, up_cols), BF16),
            pltpu.VMEM(hop_blocks.shape, BF16),
            pltpu.VMEM((low, spans, tops, block), BF16),
            pltpu.VMEM((n_lo, groups, spans, tops, block), BF16),
            pltpu.VMEM(pair, F32),
            pltpu.VMEM(pair, BF16),
            pltpu.VMEM((n_lo, block // n_hi, block), BF16),
            pltpu.VMEM((n_lo, groups, spans, tops, block), BF16),
            pltpu.VMEM((spans, low, tops, block), BF16),
            pltpu.SemaphoreType.DMA((5,)),
            pltpu.SemaphoreType.DMA((2,)),
            pltpu.SemaphoreType.DMA((2, devices)),
            pltpu.SemaphoreType.DMA((2, devices)),
        ],
        compiler_params=pltpu.CompilerParams(
            collective_id=0, has_side_effects=True, vmem_limit_bytes=48 * 1024 * 1024
        ),
        name="trotter_step",
    )(amplitudes, hop_blocks, coupling_seed)


def on_device(counts, amplitudes, hop_blocks, coupling_seed):
    n_hi, n_mid, n_lo = counts
    groups, devices = n_hi * n_mid, n_hi * n_mid * n_lo
    block = hop_blocks.shape[1]
    down_rows, up_cols = amplitudes.shape
    low = up_cols * groups // block
    fits = (
        low == devices
        and down_rows == block
        and up_cols % block == 0
        and block % (low * 16) == 0
        and block % (n_lo * 128) == 0
        and block // groups == (up_cols // block) * (block // low)
    )
    if fits:
        return by_kernel(counts, amplitudes, hop_blocks, coupling_seed)
    return by_collectives(amplitudes, hop_blocks, coupling_seed)


def solution(mesh):
    counts = tuple(mesh.shape[name] for name in AXES)
    in_specs = (P("lo", ("hi", "mid")), P(), P())
    out_specs = P("lo", ("hi", "mid"))
    return jax.shard_map(
        functools.partial(on_device, counts),
        mesh=mesh,
        in_specs=in_specs,
        out_specs=out_specs,
        check_vma=False,
    )
```

```python
import functools

import jax
import jax.numpy as jnp
from jax import lax
from jax.experimental import pallas as pl
from jax.experimental.pallas import tpu as pltpu
from jax.sharding import PartitionSpec as P

SITES = 14
COUPLING = 0.06
AXES = ("hi", "mid", "lo")
SIDES = 2
F32, BF16 = jnp.float32, jnp.bfloat16


def occupancy(indices):
    site_ids = jnp.arange(SITES, dtype=jnp.int32)
    return (indices[:, None] >> site_ids[None, :] & 1).astype(jnp.float32)


def diagonal_factor(up_index, down_index, coupling_seed):
    up_occupied = occupancy(up_index)
    down_occupied = occupancy(down_index)
    strength = COUPLING * coupling_seed.astype(jnp.float32)
    energy = jnp.dot(
        up_occupied * strength[None, :], down_occupied.T, precision=lax.Precision.HIGHEST
    )
    return jnp.exp(-energy)


def by_collectives(amplitudes, hop_blocks, coupling_seed):
    block = hop_blocks.shape[1]
    down_rows, up_cols = amplitudes.shape
    groups = lax.axis_size(("hi", "mid"))
    lo_count = lax.axis_size("lo")
    split_view = amplitudes.reshape(down_rows, up_cols // block, block)
    first_pass = jnp.einsum(
        "dav,wv->awd", split_view, hop_blocks[0], preferred_element_type=jnp.float32
    ).astype(jnp.bfloat16)
    local_top = block // groups
    remainder = up_cols // local_top
    first_pass = first_pass.reshape(local_top, remainder, down_rows)
    moved = lax.all_to_all(first_pass, ("hi", "mid"), split_axis=1, concat_axis=0, tiled=True)
    second_pass = jnp.einsum(
        "gh,hpd->gpd", hop_blocks[1], moved, preferred_element_type=jnp.float32
    )
    span_low = remainder // groups
    up_index = (
        jnp.arange(block, dtype=jnp.int32)[:, None] * remainder
        + lax.axis_index(("hi", "mid")) * span_low
        + jnp.arange(span_low, dtype=jnp.int32)[None, :]
    ).reshape(-1)
    down_index = lax.axis_index("lo") * down_rows + jnp.arange(down_rows, dtype=jnp.int32)
    factor = diagonal_factor(up_index, down_index, coupling_seed).reshape(
        block, span_low, down_rows
    )
    mixed_pass = (second_pass * factor).astype(jnp.bfloat16)
    returned = lax.all_to_all(
        mixed_pass, ("hi", "mid"), split_axis=0, concat_axis=1, tiled=True
    ).reshape(up_cols, down_rows)
    third_pass = jnp.einsum(
        "ud,ed->eu", returned, hop_blocks[2], preferred_element_type=jnp.float32
    ).astype(jnp.bfloat16)
    gathered = lax.all_to_all(
        third_pass.reshape(block // lo_count, lo_count, up_cols),
        "lo",
        split_axis=1,
        concat_axis=0,
        tiled=True,
    )
    fourth_pass = jnp.einsum(
        "gh,hpu->gpu", hop_blocks[3], gathered, preferred_element_type=jnp.float32
    ).astype(jnp.bfloat16)
    result = lax.all_to_all(fourth_pass, "lo", split_axis=0, concat_axis=1, tiled=True).reshape(
        down_rows, up_cols
    )
    return result


def dot_nn(a, b):
    return lax.dot_general(a, b, (((1,), (0,)), ((), ())), preferred_element_type=F32)


def dot_nt(a, b):
    return lax.dot_general(a, b, (((1,), (1,)), ((), ())), preferred_element_type=F32)


def ones_where(shape, condition):
    rows = lax.broadcasted_iota(jnp.int32, shape, 0)
    cols = lax.broadcasted_iota(jnp.int32, shape, 1)
    return jnp.where(condition(rows, cols), 1.0, 0.0).astype(F32).astype(BF16)


def step_kernel(
    counts,
    low,
    amp_hbm,
    hop_hbm,
    seed_ref,
    out_ref,
    amp,
    hop,
    hop0,
    hop1,
    hop2,
    hop3,
    packed,
    moved,
    factor,
    third,
    fourth,
    final,
    in_sem,
    own_sem,
    send_sem,
    recv_sem,
):
    n_hi, n_mid, n_lo = counts
    devices = n_hi * n_mid * n_lo
    groups = n_hi * n_mid
    near = groups // SIDES
    block = hop.shape[1]
    tops = block // low
    spans = amp.shape[0]
    halves = block // n_lo
    rows = near * tops
    my_hi, my_mid, my_lo = (lax.axis_index(name) for name in AXES)
    my_group = my_hi * n_mid + my_mid
    my_side = my_group // near
    me = my_group * n_lo + my_lo
    mesh_id = pl.DeviceIdType.MESH

    hop_in = [
        pltpu.make_async_copy(hop_hbm.at[k], hop.at[k], in_sem.at[k]) for k in range(4)
    ]
    amp_in = [
        pltpu.make_async_copy(
            amp_hbm.at[:, b * block : (b + 1) * block], amp.at[b], in_sem.at[4 + b]
        )
        for b in range(spans)
    ]
    hop_in[0].start()
    for copy in amp_in:
        copy.start()
    for copy in hop_in[1:]:
        copy.start()

    def spot(side_step, lo_step, k):
        side = lax.rem(my_side + side_step, SIDES)
        group = side * near + lax.rem(lax.rem(my_group, near) + k, near)
        return group, lax.rem(my_lo + lo_step, n_lo)

    def where(group, lo):
        return group // n_mid, lax.rem(group, n_mid), lo

    def each(side_step, lo_step, act):
        def body(k, carry):
            act(*spot(side_step, lo_step, k))
            return carry

        lax.fori_loop(1 if side_step == lo_step == 0 else 0, near, body, 0)

    side_steps = [*range(1, SIDES), 0]
    barrier = pltpu.get_barrier_semaphore()

    def greet(group, lo):
        pl.semaphore_signal(
            barrier, inc=1, device_id=where(group, lo), device_id_type=mesh_id
        )

    for lo_step in range(n_lo):
        for side_step in side_steps:
            each(side_step, lo_step, greet)

    def out_copy(group, lo):
        return pltpu.make_async_remote_copy(
            src_ref=packed.at[lo, group],
            dst_ref=moved.at[my_lo, my_group],
            send_sem=send_sem.at[0, group * n_lo + lo],
            recv_sem=recv_sem.at[0, me],
            device_id=where(group, lo),
            device_id_type=mesh_id,
        )

    def in_copy(group, lo):
        return pltpu.make_async_remote_copy(
            src_ref=packed.at[lo, group],
            dst_ref=moved.at[lo, group],
            send_sem=send_sem.at[0, group * n_lo + lo],
            recv_sem=recv_sem.at[0, group * n_lo + lo],
            device_id=where(group, lo),
            device_id_type=mesh_id,
        )

    def back_copy(b, group, lo):
        return pltpu.make_async_remote_copy(
            src_ref=fourth.at[lo, b, group],
            dst_ref=final.at[b, my_lo * groups + my_group],
            send_sem=send_sem.at[1 + b, group * n_lo + lo],
            recv_sem=recv_sem.at[1 + b, me],
            device_id=where(group, lo),
            device_id_type=mesh_id,
        )

    def home_copy(b, group, lo):
        return pltpu.make_async_remote_copy(
            src_ref=fourth.at[lo, b, group],
            dst_ref=final.at[b, lo * groups + group],
            send_sem=send_sem.at[1 + b, group * n_lo + lo],
            recv_sem=recv_sem.at[1 + b, group * n_lo + lo],
            device_id=where(group, lo),
            device_id_type=mesh_id,
        )

    sorter = ones_where(
        (block, block),
        lambda r, c: c == (r % tops) * low + (r // tops % groups) * n_lo + r // (tops * groups),
    )
    hop_in[0].wait()
    hop0[...] = dot_nn(sorter, hop[0]).astype(BF16).reshape(hop0.shape)
    for copy in amp_in:
        copy.wait()
    greeted = False
    for lo_step in range(n_lo):
        lo = lax.rem(my_lo + lo_step, n_lo)
        for side_step in side_steps:
            side = lax.rem(my_side + side_step, SIDES)
            for b in range(spans):
                first = dot_nt(hop0[lo, side], amp[b]).astype(BF16)
                packed[lo, pl.ds(side * near, near), b] = first.reshape(near, tops, block)
            if not greeted:
                pl.semaphore_wait(barrier, devices - 1)
                greeted = True
            each(side_step, lo_step, lambda g, l: out_copy(g, l).start())
    own_out = pltpu.make_async_copy(
        packed.at[my_lo, my_group], moved.at[my_lo, my_group], own_sem.at[0]
    )
    own_out.start()

    for copy in hop_in[1:]:
        copy.wait()
    for b in range(spans):
        hop1[b] = (
            hop[1].reshape(groups, spans, tops, block)[:, b].reshape(SIDES, rows, block)
        )
    unzip = ones_where((block, block), lambda r, c: c == (r % halves) * n_lo + r // halves)
    hop2[...] = dot_nn(unzip, hop[2]).T.astype(BF16)
    hop3[...] = hop[3].astype(F32).T.astype(BF16).reshape(hop3.shape)
    at = lax.broadcasted_iota(jnp.int32, (block, 16), 0)
    span, group, top = at // (tops * groups), at // tops % groups, at % tops
    ups = ((group * spans + span) * tops + top) * low + me
    site_r = lax.broadcasted_iota(jnp.int32, (block, 16), 1)
    strength = jnp.zeros((block, 16), F32)
    for i in range(SITES):
        strength = jnp.where(site_r == i, seed_ref[i].astype(F32), strength)
    up_part = (((ups >> site_r) & 1).astype(F32) * strength).astype(BF16)
    downs = lax.broadcasted_iota(jnp.int32, (16, n_lo * block), 1)
    site_c = lax.broadcasted_iota(jnp.int32, (16, n_lo * block), 0)
    down_part = ((downs >> site_c) & 1).astype(F32).astype(BF16)
    for lo in range(n_lo):
        part = dot_nn(up_part, down_part[:, lo * block : (lo + 1) * block])
        factor[lo] = jnp.exp(-COUPLING * part).reshape(factor.shape[1:])
    own_out.wait()

    def two_passes(lo, b, side):
        second = dot_nn(hop1[b, side], moved[lo].reshape(block, block))
        mixed = (second * factor[lo, b, side]).astype(BF16)
        return dot_nn(mixed, hop2[...]).astype(BF16)

    for lo_step in range(n_lo):
        for side_step in side_steps:
            each(side_step, lo_step, lambda g, l: in_copy(g, l).wait_recv())
        lo = lax.rem(my_lo + lo_step, n_lo)
        if lo_step < n_lo - 1:
            for b in range(spans):
                for side in range(SIDES):
                    third[lo_step, b, side] = two_passes(lo, b, side)
    last_lo = lo
    for b in range(spans):
        for side_step in side_steps:
            side = lax.rem(my_side + side_step, SIDES)
            thirds = [third[k, b, side] for k in range(n_lo - 1)]
            thirds.append(two_passes(last_lo, b, side))
            for r in range(n_lo):
                total = sum(
                    dot_nn(
                        thirds[k][:, r * halves : (r + 1) * halves],
                        hop3[lax.rem(my_lo + k, n_lo)],
                    )
                    for k in range(n_lo)
                ).astype(BF16)
                for lo in range(n_lo):
                    piece = total[:, lo * halves : (lo + 1) * halves]
                    fourth[
                        lo, b, pl.ds(side * near, near), :, r * halves : (r + 1) * halves
                    ] = piece.reshape(near, tops, halves)
            for lo_step in range(n_lo):
                each(side_step, lo_step, lambda g, l: back_copy(b, g, l).start())
    own_back = [
        pltpu.make_async_copy(
            fourth.at[my_lo, b, my_group],
            final.at[b, my_lo * groups + my_group],
            own_sem.at[1 + b],
        )
        for b in range(spans)
    ]
    for copy in own_back:
        copy.start()
    zipper = ones_where((block, block), lambda r, c: r == (c % halves) * n_lo + c // halves)
    for b in range(spans):
        own_back[b].wait()
        for lo_step in range(n_lo):
            for side_step in side_steps:
                each(side_step, lo_step, lambda g, l: home_copy(b, g, l).wait_recv())
        turned = dot_nt(zipper, final[b].reshape(block, block)).astype(BF16)
        out_ref[:, b * block : (b + 1) * block] = dot_nn(turned, sorter).astype(BF16)

    def drain(group, lo):
        out_copy(group, lo).wait_send()
        for b in range(spans):
            back_copy(b, group, lo).wait_send()

    for lo_step in range(n_lo):
        for side_step in side_steps:
            each(side_step, lo_step, drain)


def by_kernel(counts, amplitudes, hop_blocks, coupling_seed):
    n_hi, n_mid, n_lo = counts
    groups, devices = n_hi * n_mid, n_hi * n_mid * n_lo
    block = hop_blocks.shape[1]
    down_rows, up_cols = amplitudes.shape
    low = up_cols * groups // block
    tops = block // low
    spans = up_cols // block
    rows = groups // SIDES * tops
    return pl.pallas_call(
        functools.partial(step_kernel, counts, low),
        out_shape=jax.ShapeDtypeStruct((down_rows, up_cols), BF16),
        in_specs=[
            pl.BlockSpec(memory_space=pltpu.HBM),
            pl.BlockSpec(memory_space=pltpu.HBM),
            pl.BlockSpec(memory_space=pltpu.SMEM),
        ],
        out_specs=pl.BlockSpec(memory_space=pltpu.VMEM),
        scratch_shapes=[
            pltpu.VMEM((spans, block, block), BF16),
            pltpu.VMEM(hop_blocks.shape, BF16),
            pltpu.VMEM((n_lo, SIDES, rows, block), BF16),
            pltpu.VMEM((spans, SIDES, rows, block), BF16),
            pltpu.VMEM((block, block), BF16),
            pltpu.VMEM((n_lo, block // n_lo, block), BF16),
            pltpu.VMEM((n_lo, groups, spans, tops, block), BF16),
            pltpu.VMEM((n_lo, groups, spans, tops, block), BF16),
            pltpu.VMEM((n_lo, spans, SIDES, rows, block), F32),
            pltpu.VMEM((n_lo - 1, spans, SIDES, rows, block), BF16),
            pltpu.VMEM((n_lo, spans, groups, tops, block), BF16),
            pltpu.VMEM((spans, low, tops, block), BF16),
            pltpu.SemaphoreType.DMA((4 + spans,)),
            pltpu.SemaphoreType.DMA((1 + spans,)),
            pltpu.SemaphoreType.DMA((1 + spans, devices)),
            pltpu.SemaphoreType.DMA((1 + spans, devices)),
        ],
        compiler_params=pltpu.CompilerParams(
            collective_id=0, has_side_effects=True, vmem_limit_bytes=60 * 1024 * 1024
        ),
        name="trotter_step",
    )(amplitudes, hop_blocks, coupling_seed)


def on_device(counts, amplitudes, hop_blocks, coupling_seed):
    n_hi, n_mid, n_lo = counts
    groups, devices = n_hi * n_mid, n_hi * n_mid * n_lo
    block = hop_blocks.shape[1]
    down_rows, up_cols = amplitudes.shape
    low = up_cols * groups // block
    fits = (
        low == devices
        and down_rows == block
        and up_cols % block == 0
        and block % (low * 16) == 0
        and n_lo > 1
        and n_hi % SIDES == 0
        and block % (n_lo * 128) == 0
        and block // groups == (up_cols // block) * (block // low)
    )
    if fits:
        return by_kernel(counts, amplitudes, hop_blocks, coupling_seed)
    return by_collectives(amplitudes, hop_blocks, coupling_seed)


def solution(mesh):
    counts = tuple(mesh.shape[name] for name in AXES)
    in_specs = (P("lo", ("hi", "mid")), P(), P())
    out_specs = P("lo", ("hi", "mid"))
    return jax.shard_map(
        functools.partial(on_device, counts),
        mesh=mesh,
        in_specs=in_specs,
        out_specs=out_specs,
        check_vma=False,
    )
```

```python
import functools

import jax
import jax.numpy as jnp
from jax import lax
from jax.experimental import pallas as pl
from jax.experimental.pallas import tpu as pltpu
from jax.sharding import PartitionSpec as P

SITES = 14
COUPLING = 0.06
AXES = ("hi", "mid", "lo")
SIDES = 2
F32, BF16 = jnp.float32, jnp.bfloat16


def occupancy(indices):
    site_ids = jnp.arange(SITES, dtype=jnp.int32)
    return (indices[:, None] >> site_ids[None, :] & 1).astype(jnp.float32)


def diagonal_factor(up_index, down_index, coupling_seed):
    up_occupied = occupancy(up_index)
    down_occupied = occupancy(down_index)
    strength = COUPLING * coupling_seed.astype(jnp.float32)
    energy = jnp.dot(
        up_occupied * strength[None, :], down_occupied.T, precision=lax.Precision.HIGHEST
    )
    return jnp.exp(-energy)


def by_collectives(amplitudes, hop_blocks, coupling_seed):
    block = hop_blocks.shape[1]
    down_rows, up_cols = amplitudes.shape
    groups = lax.axis_size(("hi", "mid"))
    lo_count = lax.axis_size("lo")
    split_view = amplitudes.reshape(down_rows, up_cols // block, block)
    first_pass = jnp.einsum(
        "dav,wv->awd", split_view, hop_blocks[0], preferred_element_type=jnp.float32
    ).astype(jnp.bfloat16)
    local_top = block // groups
    remainder = up_cols // local_top
    first_pass = first_pass.reshape(local_top, remainder, down_rows)
    moved = lax.all_to_all(first_pass, ("hi", "mid"), split_axis=1, concat_axis=0, tiled=True)
    second_pass = jnp.einsum(
        "gh,hpd->gpd", hop_blocks[1], moved, preferred_element_type=jnp.float32
    )
    span_low = remainder // groups
    up_index = (
        jnp.arange(block, dtype=jnp.int32)[:, None] * remainder
        + lax.axis_index(("hi", "mid")) * span_low
        + jnp.arange(span_low, dtype=jnp.int32)[None, :]
    ).reshape(-1)
    down_index = lax.axis_index("lo") * down_rows + jnp.arange(down_rows, dtype=jnp.int32)
    factor = diagonal_factor(up_index, down_index, coupling_seed).reshape(
        block, span_low, down_rows
    )
    mixed_pass = (second_pass * factor).astype(jnp.bfloat16)
    returned = lax.all_to_all(
        mixed_pass, ("hi", "mid"), split_axis=0, concat_axis=1, tiled=True
    ).reshape(up_cols, down_rows)
    third_pass = jnp.einsum(
        "ud,ed->eu", returned, hop_blocks[2], preferred_element_type=jnp.float32
    ).astype(jnp.bfloat16)
    gathered = lax.all_to_all(
        third_pass.reshape(block // lo_count, lo_count, up_cols),
        "lo",
        split_axis=1,
        concat_axis=0,
        tiled=True,
    )
    fourth_pass = jnp.einsum(
        "gh,hpu->gpu", hop_blocks[3], gathered, preferred_element_type=jnp.float32
    ).astype(jnp.bfloat16)
    result = lax.all_to_all(fourth_pass, "lo", split_axis=0, concat_axis=1, tiled=True).reshape(
        down_rows, up_cols
    )
    return result


def dot_nn(a, b):
    return lax.dot_general(a, b, (((1,), (0,)), ((), ())), preferred_element_type=F32)


def dot_nt(a, b):
    return lax.dot_general(a, b, (((1,), (1,)), ((), ())), preferred_element_type=F32)


def ones_where(shape, condition):
    rows = lax.broadcasted_iota(jnp.int32, shape, 0)
    cols = lax.broadcasted_iota(jnp.int32, shape, 1)
    return jnp.where(condition(rows, cols), 1.0, 0.0).astype(F32).astype(BF16)


def step_kernel(
    counts,
    low,
    amp_hbm,
    hop_hbm,
    seed_ref,
    out_ref,
    amp,
    hop,
    hop0,
    hop1,
    hop2,
    hop3,
    packed,
    moved,
    factor,
    third,
    fourth,
    final,
    in_sem,
    own_sem,
    send_sem,
    recv_sem,
):
    n_hi, n_mid, n_lo = counts
    devices = n_hi * n_mid * n_lo
    groups = n_hi * n_mid
    near = groups // SIDES
    block = hop.shape[1]
    tops = block // low
    spans = amp.shape[0]
    halves = block // n_lo
    rows = near * tops
    my_hi, my_mid, my_lo = (lax.axis_index(name) for name in AXES)
    my_group = my_hi * n_mid + my_mid
    my_side = my_group // near
    me = my_group * n_lo + my_lo
    mesh_id = pl.DeviceIdType.MESH

    hop_in = [
        pltpu.make_async_copy(hop_hbm.at[k], hop.at[k], in_sem.at[k]) for k in range(4)
    ]
    amp_in = [
        pltpu.make_async_copy(
            amp_hbm.at[:, b * block : (b + 1) * block], amp.at[b], in_sem.at[4 + b]
        )
        for b in range(spans)
    ]
    hop_in[0].start()
    for copy in amp_in:
        copy.start()
    for copy in hop_in[1:]:
        copy.start()

    def spot(side_step, lo_step, k):
        side = lax.rem(my_side + side_step, SIDES)
        group = side * near + lax.rem(lax.rem(my_group, near) + k, near)
        return group, lax.rem(my_lo + lo_step, n_lo)

    def where(group, lo):
        return group // n_mid, lax.rem(group, n_mid), lo

    def each(side_step, lo_step, act):
        def body(k, carry):
            act(*spot(side_step, lo_step, k))
            return carry

        lax.fori_loop(1 if side_step == lo_step == 0 else 0, near, body, 0)

    side_steps = [*range(1, SIDES), 0]
    barrier = pltpu.get_barrier_semaphore()

    def greet(group, lo):
        pl.semaphore_signal(
            barrier, inc=1, device_id=where(group, lo), device_id_type=mesh_id
        )

    for lo_step in range(n_lo):
        for side_step in side_steps:
            each(side_step, lo_step, greet)

    def out_copy(group, lo):
        return pltpu.make_async_remote_copy(
            src_ref=packed.at[lo, group],
            dst_ref=moved.at[my_lo, my_group],
            send_sem=send_sem.at[0, group * n_lo + lo],
            recv_sem=recv_sem.at[0, me],
            device_id=where(group, lo),
            device_id_type=mesh_id,
        )

    def in_copy(group, lo):
        return pltpu.make_async_remote_copy(
            src_ref=packed.at[lo, group],
            dst_ref=moved.at[lo, group],
            send_sem=send_sem.at[0, group * n_lo + lo],
            recv_sem=recv_sem.at[0, group * n_lo + lo],
            device_id=where(group, lo),
            device_id_type=mesh_id,
        )

    def back_copy(b, group, lo):
        return pltpu.make_async_remote_copy(
            src_ref=fourth.at[lo, b, group],
            dst_ref=final.at[b, my_lo * groups + my_group],
            send_sem=send_sem.at[1 + b, group * n_lo + lo],
            recv_sem=recv_sem.at[1 + b, me],
            device_id=where(group, lo),
            device_id_type=mesh_id,
        )

    def home_copy(b, group, lo):
        return pltpu.make_async_remote_copy(
            src_ref=fourth.at[lo, b, group],
            dst_ref=final.at[b, lo * groups + group],
            send_sem=send_sem.at[1 + b, group * n_lo + lo],
            recv_sem=recv_sem.at[1 + b, group * n_lo + lo],
            device_id=where(group, lo),
            device_id_type=mesh_id,
        )

    sorter = ones_where(
        (block, block),
        lambda r, c: c == (r % tops) * low + (r // tops % groups) * n_lo + r // (tops * groups),
    )
    hop_in[0].wait()
    hop0[...] = dot_nn(sorter, hop[0]).astype(BF16).reshape(hop0.shape)
    for copy in amp_in:
        copy.wait()
    greeted = False
    for side_step in side_steps:
        side = lax.rem(my_side + side_step, SIDES)
        for lo_step in range(n_lo):
            lo = lax.rem(my_lo + lo_step, n_lo)
            for b in range(spans):
                first = dot_nt(hop0[lo, side], amp[b]).astype(BF16)
                packed[lo, pl.ds(side * near, near), b] = first.reshape(near, tops, block)
            if not greeted:
                pl.semaphore_wait(barrier, devices - 1)
                greeted = True
            each(side_step, lo_step, lambda g, l: out_copy(g, l).start())
    own_out = pltpu.make_async_copy(
        packed.at[my_lo, my_group], moved.at[my_lo, my_group], own_sem.at[0]
    )
    own_out.start()

    for copy in hop_in[1:]:
        copy.wait()
    for b in range(spans):
        hop1[b] = (
            hop[1].reshape(groups, spans, tops, block)[:, b].reshape(SIDES, rows, block)
        )
    unzip = ones_where((block, block), lambda r, c: c == (r % halves) * n_lo + r // halves)
    hop2[...] = dot_nn(unzip, hop[2]).T.astype(BF16)
    hop3[...] = hop[3].astype(F32).T.astype(BF16).reshape(hop3.shape)
    at = lax.broadcasted_iota(jnp.int32, (block, 16), 0)
    span, group, top = at // (tops * groups), at // tops % groups, at % tops
    ups = ((group * spans + span) * tops + top) * low + me
    site_r = lax.broadcasted_iota(jnp.int32, (block, 16), 1)
    strength = jnp.zeros((block, 16), F32)
    for i in range(SITES):
        strength = jnp.where(site_r == i, seed_ref[i].astype(F32), strength)
    up_part = (((ups >> site_r) & 1).astype(F32) * strength).astype(BF16)
    downs = lax.broadcasted_iota(jnp.int32, (16, n_lo * block), 1)
    site_c = lax.broadcasted_iota(jnp.int32, (16, n_lo * block), 0)
    down_part = ((downs >> site_c) & 1).astype(F32).astype(BF16)
    for lo in range(n_lo):
        part = dot_nn(up_part, down_part[:, lo * block : (lo + 1) * block])
        factor[lo] = jnp.exp(-COUPLING * part).reshape(factor.shape[1:])
    own_out.wait()

    def two_passes(lo, b, side):
        second = dot_nn(hop1[b, side], moved[lo].reshape(block, block))
        mixed = (second * factor[lo, b, side]).astype(BF16)
        return dot_nn(mixed, hop2[...]).astype(BF16)

    for lo_step in range(n_lo):
        for side_step in side_steps:
            each(side_step, lo_step, lambda g, l: in_copy(g, l).wait_recv())
        lo = lax.rem(my_lo + lo_step, n_lo)
        if lo_step < n_lo - 1:
            for b in range(spans):
                for side in range(SIDES):
                    third[lo_step, b, side] = two_passes(lo, b, side)
    last_lo = lo
    for side_step in side_steps:
        for b in range(spans):
            side = lax.rem(my_side + side_step, SIDES)
            thirds = [third[k, b, side] for k in range(n_lo - 1)]
            thirds.append(two_passes(last_lo, b, side))
            for r in range(n_lo):
                total = sum(
                    dot_nn(
                        thirds[k][:, r * halves : (r + 1) * halves],
                        hop3[lax.rem(my_lo + k, n_lo)],
                    )
                    for k in range(n_lo)
                ).astype(BF16)
                for lo in range(n_lo):
                    piece = total[:, lo * halves : (lo + 1) * halves]
                    fourth[
                        lo, b, pl.ds(side * near, near), :, r * halves : (r + 1) * halves
                    ] = piece.reshape(near, tops, halves)
            for lo_step in range(n_lo):
                each(side_step, lo_step, lambda g, l: back_copy(b, g, l).start())
    own_back = [
        pltpu.make_async_copy(
            fourth.at[my_lo, b, my_group],
            final.at[b, my_lo * groups + my_group],
            own_sem.at[1 + b],
        )
        for b in range(spans)
    ]
    for copy in own_back:
        copy.start()
    zipper = ones_where((block, block), lambda r, c: r == (c % halves) * n_lo + c // halves)
    for b in range(spans):
        own_back[b].wait()
        for lo_step in range(n_lo):
            for side_step in side_steps:
                each(side_step, lo_step, lambda g, l: home_copy(b, g, l).wait_recv())
        turned = dot_nt(zipper, final[b].reshape(block, block)).astype(BF16)
        out_ref[:, b * block : (b + 1) * block] = dot_nn(turned, sorter).astype(BF16)

    def drain(group, lo):
        out_copy(group, lo).wait_send()
        for b in range(spans):
            back_copy(b, group, lo).wait_send()

    for lo_step in range(n_lo):
        for side_step in side_steps:
            each(side_step, lo_step, drain)


def by_kernel(counts, amplitudes, hop_blocks, coupling_seed):
    n_hi, n_mid, n_lo = counts
    groups, devices = n_hi * n_mid, n_hi * n_mid * n_lo
    block = hop_blocks.shape[1]
    down_rows, up_cols = amplitudes.shape
    low = up_cols * groups // block
    tops = block // low
    spans = up_cols // block
    rows = groups // SIDES * tops
    return pl.pallas_call(
        functools.partial(step_kernel, counts, low),
        out_shape=jax.ShapeDtypeStruct((down_rows, up_cols), BF16),
        in_specs=[
            pl.BlockSpec(memory_space=pltpu.HBM),
            pl.BlockSpec(memory_space=pltpu.HBM),
            pl.BlockSpec(memory_space=pltpu.SMEM),
        ],
        out_specs=pl.BlockSpec(memory_space=pltpu.VMEM),
        scratch_shapes=[
            pltpu.VMEM((spans, block, block), BF16),
            pltpu.VMEM(hop_blocks.shape, BF16),
            pltpu.VMEM((n_lo, SIDES, rows, block), BF16),
            pltpu.VMEM((spans, SIDES, rows, block), BF16),
            pltpu.VMEM((block, block), BF16),
            pltpu.VMEM((n_lo, block // n_lo, block), BF16),
            pltpu.VMEM((n_lo, groups, spans, tops, block), BF16),
            pltpu.VMEM((n_lo, groups, spans, tops, block), BF16),
            pltpu.VMEM((n_lo, spans, SIDES, rows, block), F32),
            pltpu.VMEM((n_lo - 1, spans, SIDES, rows, block), BF16),
            pltpu.VMEM((n_lo, spans, groups, tops, block), BF16),
            pltpu.VMEM((spans, low, tops, block), BF16),
            pltpu.SemaphoreType.DMA((4 + spans,)),
            pltpu.SemaphoreType.DMA((1 + spans,)),
            pltpu.SemaphoreType.DMA((1 + spans, devices)),
            pltpu.SemaphoreType.DMA((1 + spans, devices)),
        ],
        compiler_params=pltpu.CompilerParams(
            collective_id=0, has_side_effects=True, vmem_limit_bytes=60 * 1024 * 1024
        ),
        name="trotter_step",
    )(amplitudes, hop_blocks, coupling_seed)


def on_device(counts, amplitudes, hop_blocks, coupling_seed):
    n_hi, n_mid, n_lo = counts
    groups, devices = n_hi * n_mid, n_hi * n_mid * n_lo
    block = hop_blocks.shape[1]
    down_rows, up_cols = amplitudes.shape
    low = up_cols * groups // block
    fits = (
        low == devices
        and down_rows == block
        and up_cols % block == 0
        and block % (low * 16) == 0
        and n_lo > 1
        and n_hi % SIDES == 0
        and block % (n_lo * 128) == 0
        and block // groups == (up_cols // block) * (block // low)
    )
    if fits:
        return by_kernel(counts, amplitudes, hop_blocks, coupling_seed)
    return by_collectives(amplitudes, hop_blocks, coupling_seed)


def solution(mesh):
    counts = tuple(mesh.shape[name] for name in AXES)
    in_specs = (P("lo", ("hi", "mid")), P(), P())
    out_specs = P("lo", ("hi", "mid"))
    return jax.shard_map(
        functools.partial(on_device, counts),
        mesh=mesh,
        in_specs=in_specs,
        out_specs=out_specs,
        check_vma=False,
    )
```

```python
import functools

import jax
import jax.numpy as jnp
from jax import lax
from jax.experimental import pallas as pl
from jax.experimental.pallas import tpu as pltpu
from jax.sharding import PartitionSpec as P

SITES = 14
COUPLING = 0.06
AXES = ("hi", "mid", "lo")
SIDES = 2
F32, BF16 = jnp.float32, jnp.bfloat16


def occupancy(indices):
    site_ids = jnp.arange(SITES, dtype=jnp.int32)
    return (indices[:, None] >> site_ids[None, :] & 1).astype(jnp.float32)


def diagonal_factor(up_index, down_index, coupling_seed):
    up_occupied = occupancy(up_index)
    down_occupied = occupancy(down_index)
    strength = COUPLING * coupling_seed.astype(jnp.float32)
    energy = jnp.dot(
        up_occupied * strength[None, :], down_occupied.T, precision=lax.Precision.HIGHEST
    )
    return jnp.exp(-energy)


def by_collectives(amplitudes, hop_blocks, coupling_seed):
    block = hop_blocks.shape[1]
    down_rows, up_cols = amplitudes.shape
    groups = lax.axis_size(("hi", "mid"))
    lo_count = lax.axis_size("lo")
    split_view = amplitudes.reshape(down_rows, up_cols // block, block)
    first_pass = jnp.einsum(
        "dav,wv->awd", split_view, hop_blocks[0], preferred_element_type=jnp.float32
    ).astype(jnp.bfloat16)
    local_top = block // groups
    remainder = up_cols // local_top
    first_pass = first_pass.reshape(local_top, remainder, down_rows)
    moved = lax.all_to_all(first_pass, ("hi", "mid"), split_axis=1, concat_axis=0, tiled=True)
    second_pass = jnp.einsum(
        "gh,hpd->gpd", hop_blocks[1], moved, preferred_element_type=jnp.float32
    )
    span_low = remainder // groups
    up_index = (
        jnp.arange(block, dtype=jnp.int32)[:, None] * remainder
        + lax.axis_index(("hi", "mid")) * span_low
        + jnp.arange(span_low, dtype=jnp.int32)[None, :]
    ).reshape(-1)
    down_index = lax.axis_index("lo") * down_rows + jnp.arange(down_rows, dtype=jnp.int32)
    factor = diagonal_factor(up_index, down_index, coupling_seed).reshape(
        block, span_low, down_rows
    )
    mixed_pass = (second_pass * factor).astype(jnp.bfloat16)
    returned = lax.all_to_all(
        mixed_pass, ("hi", "mid"), split_axis=0, concat_axis=1, tiled=True
    ).reshape(up_cols, down_rows)
    third_pass = jnp.einsum(
        "ud,ed->eu", returned, hop_blocks[2], preferred_element_type=jnp.float32
    ).astype(jnp.bfloat16)
    gathered = lax.all_to_all(
        third_pass.reshape(block // lo_count, lo_count, up_cols),
        "lo",
        split_axis=1,
        concat_axis=0,
        tiled=True,
    )
    fourth_pass = jnp.einsum(
        "gh,hpu->gpu", hop_blocks[3], gathered, preferred_element_type=jnp.float32
    ).astype(jnp.bfloat16)
    result = lax.all_to_all(fourth_pass, "lo", split_axis=0, concat_axis=1, tiled=True).reshape(
        down_rows, up_cols
    )
    return result


def dot_nn(a, b):
    return lax.dot_general(a, b, (((1,), (0,)), ((), ())), preferred_element_type=F32)


def dot_nt(a, b):
    return lax.dot_general(a, b, (((1,), (1,)), ((), ())), preferred_element_type=F32)


def ones_where(shape, condition):
    rows = lax.broadcasted_iota(jnp.int32, shape, 0)
    cols = lax.broadcasted_iota(jnp.int32, shape, 1)
    return jnp.where(condition(rows, cols), 1.0, 0.0).astype(F32).astype(BF16)


def step_kernel(
    counts,
    low,
    amp_hbm,
    hop_hbm,
    seed_ref,
    out_ref,
    amp,
    hop,
    hop1,
    hop2,
    hop3,
    packed,
    moved,
    factor,
    third,
    fourth,
    final,
    in_sem,
    own_sem,
    send_sem,
    recv_sem,
):
    n_hi, n_mid, n_lo = counts
    devices = n_hi * n_mid * n_lo
    groups = n_hi * n_mid
    near = groups // SIDES
    block = hop.shape[1]
    tops = block // low
    spans = amp.shape[0]
    halves = block // n_lo
    rows = near * tops
    my_hi, my_mid, my_lo = (lax.axis_index(name) for name in AXES)
    my_group = my_hi * n_mid + my_mid
    my_side = my_group // near
    me = my_group * n_lo + my_lo
    mesh_id = pl.DeviceIdType.MESH

    hop_in = [
        pltpu.make_async_copy(hop_hbm.at[k], hop.at[k], in_sem.at[k]) for k in range(4)
    ]
    amp_in = [
        pltpu.make_async_copy(
            amp_hbm.at[:, b * block : (b + 1) * block], amp.at[b], in_sem.at[4 + b]
        )
        for b in range(spans)
    ]
    hop_in[0].start()
    for copy in amp_in:
        copy.start()

    def spot(side_step, lo_step, k):
        side = lax.rem(my_side + side_step, SIDES)
        group = side * near + lax.rem(lax.rem(my_group, near) + k, near)
        return group, lax.rem(my_lo + lo_step, n_lo)

    def where(group, lo):
        return group // n_mid, lax.rem(group, n_mid), lo

    def each(side_step, lo_step, act):
        def body(k, carry):
            act(*spot(side_step, lo_step, k))
            return carry

        lax.fori_loop(1 if side_step == lo_step == 0 else 0, near, body, 0)

    side_steps = [*range(1, SIDES), 0]
    barrier = pltpu.get_barrier_semaphore()

    def greet(group, lo):
        pl.semaphore_signal(
            barrier, inc=1, device_id=where(group, lo), device_id_type=mesh_id
        )

    for lo_step in range(n_lo):
        for side_step in side_steps:
            each(side_step, lo_step, greet)

    def out_copy(group, lo):
        return pltpu.make_async_remote_copy(
            src_ref=packed.at[lo, group],
            dst_ref=moved.at[my_lo, my_group],
            send_sem=send_sem.at[0, group * n_lo + lo],
            recv_sem=recv_sem.at[0, me],
            device_id=where(group, lo),
            device_id_type=mesh_id,
        )

    def in_copy(group, lo):
        return pltpu.make_async_remote_copy(
            src_ref=packed.at[lo, group],
            dst_ref=moved.at[lo, group],
            send_sem=send_sem.at[0, group * n_lo + lo],
            recv_sem=recv_sem.at[0, group * n_lo + lo],
            device_id=where(group, lo),
            device_id_type=mesh_id,
        )

    def back_copy(b, group, lo):
        return pltpu.make_async_remote_copy(
            src_ref=fourth.at[lo, b, group],
            dst_ref=final.at[b, my_lo * groups + my_group],
            send_sem=send_sem.at[1 + b, group * n_lo + lo],
            recv_sem=recv_sem.at[1 + b, me],
            device_id=where(group, lo),
            device_id_type=mesh_id,
        )

    def home_copy(b, group, lo):
        return pltpu.make_async_remote_copy(
            src_ref=fourth.at[lo, b, group],
            dst_ref=final.at[b, lo * groups + group],
            send_sem=send_sem.at[1 + b, group * n_lo + lo],
            recv_sem=recv_sem.at[1 + b, group * n_lo + lo],
            device_id=where(group, lo),
            device_id_type=mesh_id,
        )

    hop_in[0].wait()
    greeted = False
    for side_step in side_steps:
        side = lax.rem(my_side + side_step, SIDES)
        for lo_step in range(n_lo):
            lo = lax.rem(my_lo + lo_step, n_lo)
            picker = ones_where(
                (rows, block),
                lambda r, c: c == (r % tops) * low + (side * near + r // tops) * n_lo + lo,
            )
            weights = dot_nn(picker, hop[0]).astype(BF16)
            for b in range(spans):
                if not greeted:
                    amp_in[b].wait()
                first = dot_nt(weights, amp[b]).astype(BF16)
                packed[lo, pl.ds(side * near, near), b] = first.reshape(near, tops, block)
            if not greeted:
                pl.semaphore_wait(barrier, devices - 1)
                greeted = True
                for copy in hop_in[1:]:
                    copy.start()
            each(side_step, lo_step, lambda g, l: out_copy(g, l).start())
    own_out = pltpu.make_async_copy(
        packed.at[my_lo, my_group], moved.at[my_lo, my_group], own_sem.at[0]
    )
    own_out.start()

    for copy in hop_in[1:]:
        copy.wait()
    for b in range(spans):
        hop1[b] = (
            hop[1].reshape(groups, spans, tops, block)[:, b].reshape(SIDES, rows, block)
        )
    unzip = ones_where((block, block), lambda r, c: c == (r % halves) * n_lo + r // halves)
    hop2[...] = dot_nn(unzip, hop[2]).T.astype(BF16)
    hop3[...] = hop[3].astype(F32).T.astype(BF16).reshape(hop3.shape)
    at = lax.broadcasted_iota(jnp.int32, (block, 16), 0)
    span, group, top = at // (tops * groups), at // tops % groups, at % tops
    ups = ((group * spans + span) * tops + top) * low + me
    site_r = lax.broadcasted_iota(jnp.int32, (block, 16), 1)
    strength = jnp.zeros((block, 16), F32)
    for i in range(SITES):
        strength = jnp.where(site_r == i, seed_ref[i].astype(F32), strength)
    up_part = (((ups >> site_r) & 1).astype(F32) * strength).astype(BF16)
    downs = lax.broadcasted_iota(jnp.int32, (16, n_lo * block), 1)
    site_c = lax.broadcasted_iota(jnp.int32, (16, n_lo * block), 0)
    down_part = ((downs >> site_c) & 1).astype(F32).astype(BF16)
    for lo in range(n_lo):
        part = dot_nn(up_part, down_part[:, lo * block : (lo + 1) * block])
        factor[lo] = jnp.exp(-COUPLING * part).reshape(factor.shape[1:])
    own_out.wait()

    def two_passes(lo, b, side):
        second = dot_nn(hop1[b, side], moved[lo].reshape(block, block))
        mixed = (second * factor[lo, b, side]).astype(BF16)
        return dot_nn(mixed, hop2[...]).astype(BF16)

    for lo_step in range(n_lo):
        for side_step in side_steps:
            each(side_step, lo_step, lambda g, l: in_copy(g, l).wait_recv())
        lo = lax.rem(my_lo + lo_step, n_lo)
        if lo_step < n_lo - 1:
            for b in range(spans):
                for side in range(SIDES):
                    third[lo_step, b, side] = two_passes(lo, b, side)
    last_lo = lo
    for side_step in side_steps:
        for b in range(spans):
            side = lax.rem(my_side + side_step, SIDES)
            thirds = [third[k, b, side] for k in range(n_lo - 1)]
            thirds.append(two_passes(last_lo, b, side))
            for r in range(n_lo):
                total = sum(
                    dot_nn(
                        thirds[k][:, r * halves : (r + 1) * halves],
                        hop3[lax.rem(my_lo + k, n_lo)],
                    )
                    for k in range(n_lo)
                ).astype(BF16)
                for lo in range(n_lo):
                    piece = total[:, lo * halves : (lo + 1) * halves]
                    fourth[
                        lo, b, pl.ds(side * near, near), :, r * halves : (r + 1) * halves
                    ] = piece.reshape(near, tops, halves)
            for lo_step in range(n_lo):
                each(side_step, lo_step, lambda g, l: back_copy(b, g, l).start())
    own_back = [
        pltpu.make_async_copy(
            fourth.at[my_lo, b, my_group],
            final.at[b, my_lo * groups + my_group],
            own_sem.at[1 + b],
        )
        for b in range(spans)
    ]
    for copy in own_back:
        copy.start()
    sorter = ones_where(
        (block, block),
        lambda r, c: c == (r % tops) * low + (r // tops % groups) * n_lo + r // (tops * groups),
    )
    zipper = ones_where((block, block), lambda r, c: r == (c % halves) * n_lo + c // halves)
    for b in range(spans):
        own_back[b].wait()
        for lo_step in range(n_lo):
            for side_step in side_steps:
                each(side_step, lo_step, lambda g, l: home_copy(b, g, l).wait_recv())
        turned = dot_nt(zipper, final[b].reshape(block, block)).astype(BF16)
        out_ref[:, b * block : (b + 1) * block] = dot_nn(turned, sorter).astype(BF16)

    def drain(group, lo):
        out_copy(group, lo).wait_send()
        for b in range(spans):
            back_copy(b, group, lo).wait_send()

    for lo_step in range(n_lo):
        for side_step in side_steps:
            each(side_step, lo_step, drain)


def by_kernel(counts, amplitudes, hop_blocks, coupling_seed):
    n_hi, n_mid, n_lo = counts
    groups, devices = n_hi * n_mid, n_hi * n_mid * n_lo
    block = hop_blocks.shape[1]
    down_rows, up_cols = amplitudes.shape
    low = up_cols * groups // block
    tops = block // low
    spans = up_cols // block
    rows = groups // SIDES * tops
    return pl.pallas_call(
        functools.partial(step_kernel, counts, low),
        out_shape=jax.ShapeDtypeStruct((down_rows, up_cols), BF16),
        in_specs=[
            pl.BlockSpec(memory_space=pltpu.HBM),
            pl.BlockSpec(memory_space=pltpu.HBM),
            pl.BlockSpec(memory_space=pltpu.SMEM),
        ],
        out_specs=pl.BlockSpec(memory_space=pltpu.VMEM),
        scratch_shapes=[
            pltpu.VMEM((spans, block, block), BF16),
            pltpu.VMEM(hop_blocks.shape, BF16),
            pltpu.VMEM((spans, SIDES, rows, block), BF16),
            pltpu.VMEM((block, block), BF16),
            pltpu.VMEM((n_lo, block // n_lo, block), BF16),
            pltpu.VMEM((n_lo, groups, spans, tops, block), BF16),
            pltpu.VMEM((n_lo, groups, spans, tops, block), BF16),
            pltpu.VMEM((n_lo, spans, SIDES, rows, block), F32),
            pltpu.VMEM((n_lo - 1, spans, SIDES, rows, block), BF16),
            pltpu.VMEM((n_lo, spans, groups, tops, block), BF16),
            pltpu.VMEM((spans, low, tops, block), BF16),
            pltpu.SemaphoreType.DMA((4 + spans,)),
            pltpu.SemaphoreType.DMA((1 + spans,)),
            pltpu.SemaphoreType.DMA((1 + spans, devices)),
            pltpu.SemaphoreType.DMA((1 + spans, devices)),
        ],
        compiler_params=pltpu.CompilerParams(
            collective_id=0, has_side_effects=True, vmem_limit_bytes=60 * 1024 * 1024
        ),
        name="trotter_step",
    )(amplitudes, hop_blocks, coupling_seed)


def on_device(counts, amplitudes, hop_blocks, coupling_seed):
    n_hi, n_mid, n_lo = counts
    groups, devices = n_hi * n_mid, n_hi * n_mid * n_lo
    block = hop_blocks.shape[1]
    down_rows, up_cols = amplitudes.shape
    low = up_cols * groups // block
    fits = (
        low == devices
        and down_rows == block
        and up_cols % block == 0
        and block % (low * 16) == 0
        and n_lo > 1
        and n_hi % SIDES == 0
        and block % (n_lo * 128) == 0
        and block // groups == (up_cols // block) * (block // low)
    )
    if fits:
        return by_kernel(counts, amplitudes, hop_blocks, coupling_seed)
    return by_collectives(amplitudes, hop_blocks, coupling_seed)


def solution(mesh):
    counts = tuple(mesh.shape[name] for name in AXES)
    in_specs = (P("lo", ("hi", "mid")), P(), P())
    out_specs = P("lo", ("hi", "mid"))
    return jax.shard_map(
        functools.partial(on_device, counts),
        mesh=mesh,
        in_specs=in_specs,
        out_specs=out_specs,
        check_vma=False,
    )
```

```python
import functools

import jax
import jax.numpy as jnp
from jax import lax
from jax.experimental import pallas as pl
from jax.experimental.pallas import tpu as pltpu
from jax.sharding import PartitionSpec as P

SITES = 14
COUPLING = 0.06
AXES = ("hi", "mid", "lo")
SIDES = 2
F32, BF16 = jnp.float32, jnp.bfloat16


def occupancy(indices):
    site_ids = jnp.arange(SITES, dtype=jnp.int32)
    return (indices[:, None] >> site_ids[None, :] & 1).astype(jnp.float32)


def diagonal_factor(up_index, down_index, coupling_seed):
    up_occupied = occupancy(up_index)
    down_occupied = occupancy(down_index)
    strength = COUPLING * coupling_seed.astype(jnp.float32)
    energy = jnp.dot(
        up_occupied * strength[None, :], down_occupied.T, precision=lax.Precision.HIGHEST
    )
    return jnp.exp(-energy)


def by_collectives(amplitudes, hop_blocks, coupling_seed):
    block = hop_blocks.shape[1]
    down_rows, up_cols = amplitudes.shape
    groups = lax.axis_size(("hi", "mid"))
    lo_count = lax.axis_size("lo")
    split_view = amplitudes.reshape(down_rows, up_cols // block, block)
    first_pass = jnp.einsum(
        "dav,wv->awd", split_view, hop_blocks[0], preferred_element_type=jnp.float32
    ).astype(jnp.bfloat16)
    local_top = block // groups
    remainder = up_cols // local_top
    first_pass = first_pass.reshape(local_top, remainder, down_rows)
    moved = lax.all_to_all(first_pass, ("hi", "mid"), split_axis=1, concat_axis=0, tiled=True)
    second_pass = jnp.einsum(
        "gh,hpd->gpd", hop_blocks[1], moved, preferred_element_type=jnp.float32
    )
    span_low = remainder // groups
    up_index = (
        jnp.arange(block, dtype=jnp.int32)[:, None] * remainder
        + lax.axis_index(("hi", "mid")) * span_low
        + jnp.arange(span_low, dtype=jnp.int32)[None, :]
    ).reshape(-1)
    down_index = lax.axis_index("lo") * down_rows + jnp.arange(down_rows, dtype=jnp.int32)
    factor = diagonal_factor(up_index, down_index, coupling_seed).reshape(
        block, span_low, down_rows
    )
    mixed_pass = (second_pass * factor).astype(jnp.bfloat16)
    returned = lax.all_to_all(
        mixed_pass, ("hi", "mid"), split_axis=0, concat_axis=1, tiled=True
    ).reshape(up_cols, down_rows)
    third_pass = jnp.einsum(
        "ud,ed->eu", returned, hop_blocks[2], preferred_element_type=jnp.float32
    ).astype(jnp.bfloat16)
    gathered = lax.all_to_all(
        third_pass.reshape(block // lo_count, lo_count, up_cols),
        "lo",
        split_axis=1,
        concat_axis=0,
        tiled=True,
    )
    fourth_pass = jnp.einsum(
        "gh,hpu->gpu", hop_blocks[3], gathered, preferred_element_type=jnp.float32
    ).astype(jnp.bfloat16)
    result = lax.all_to_all(fourth_pass, "lo", split_axis=0, concat_axis=1, tiled=True).reshape(
        down_rows, up_cols
    )
    return result


def dot_nn(a, b):
    return lax.dot_general(a, b, (((1,), (0,)), ((), ())), preferred_element_type=F32)


def dot_nt(a, b):
    return lax.dot_general(a, b, (((1,), (1,)), ((), ())), preferred_element_type=F32)


def ones_where(shape, condition):
    rows = lax.broadcasted_iota(jnp.int32, shape, 0)
    cols = lax.broadcasted_iota(jnp.int32, shape, 1)
    return jnp.where(condition(rows, cols), 1.0, 0.0).astype(F32).astype(BF16)


def step_kernel(
    counts,
    low,
    amp_hbm,
    hop_hbm,
    seed_ref,
    out_ref,
    amp,
    hop,
    hop0,
    hop1,
    hop2,
    hop3,
    packed,
    moved,
    factor,
    third,
    fourth,
    final,
    in_sem,
    own_sem,
    send_sem,
    recv_sem,
):
    n_hi, n_mid, n_lo = counts
    devices = n_hi * n_mid * n_lo
    groups = n_hi * n_mid
    near = groups // SIDES
    block = hop.shape[1]
    tops = block // low
    spans = amp.shape[0]
    halves = block // n_lo
    rows = near * tops
    my_hi, my_mid, my_lo = (lax.axis_index(name) for name in AXES)
    my_group = my_hi * n_mid + my_mid
    my_side = my_group // near
    me = my_group * n_lo + my_lo
    mesh_id = pl.DeviceIdType.MESH

    hop_in = [
        pltpu.make_async_copy(hop_hbm.at[k], hop.at[k], in_sem.at[k]) for k in range(4)
    ]
    amp_in = [
        pltpu.make_async_copy(
            amp_hbm.at[:, b * block : (b + 1) * block], amp.at[b], in_sem.at[4 + b]
        )
        for b in range(spans)
    ]
    hop_in[0].start()
    for copy in amp_in:
        copy.start()
    for copy in hop_in[1:]:
        copy.start()

    def spot(side_step, lo_step, k):
        group = lax.bitwise_xor(my_group, side_step * near + k)
        return group, lax.rem(my_lo + lo_step, n_lo)

    def where(group, lo):
        return group // n_mid, lax.rem(group, n_mid), lo

    def each(side_step, lo_step, act, begin=0, end=near):
        def body(k, carry):
            act(*spot(side_step, lo_step, k))
            return carry

        if side_step == lo_step == 0:
            begin = max(begin, 1)
        lax.fori_loop(begin, end, body, 0)

    side_steps = [*range(1, SIDES), 0]
    barrier = pltpu.get_barrier_semaphore()

    def greet(group, lo):
        pl.semaphore_signal(
            barrier, inc=1, device_id=where(group, lo), device_id_type=mesh_id
        )

    for lo_step in range(n_lo):
        for side_step in side_steps:
            each(side_step, lo_step, greet)

    def out_copy(group, lo):
        return pltpu.make_async_remote_copy(
            src_ref=packed.at[lo, group],
            dst_ref=moved.at[my_lo, my_group],
            send_sem=send_sem.at[0, group * n_lo + lo],
            recv_sem=recv_sem.at[0, me],
            device_id=where(group, lo),
            device_id_type=mesh_id,
        )

    def in_copy(group, lo):
        return pltpu.make_async_remote_copy(
            src_ref=packed.at[lo, group],
            dst_ref=moved.at[lo, group],
            send_sem=send_sem.at[0, group * n_lo + lo],
            recv_sem=recv_sem.at[0, group * n_lo + lo],
            device_id=where(group, lo),
            device_id_type=mesh_id,
        )

    def back_copy(b, group, lo):
        return pltpu.make_async_remote_copy(
            src_ref=fourth.at[lo, b, group],
            dst_ref=final.at[b, my_lo * groups + my_group],
            send_sem=send_sem.at[1 + b, group * n_lo + lo],
            recv_sem=recv_sem.at[1 + b, me],
            device_id=where(group, lo),
            device_id_type=mesh_id,
        )

    def home_copy(b, group, lo):
        return pltpu.make_async_remote_copy(
            src_ref=fourth.at[lo, b, group],
            dst_ref=final.at[b, lo * groups + group],
            send_sem=send_sem.at[1 + b, group * n_lo + lo],
            recv_sem=recv_sem.at[1 + b, group * n_lo + lo],
            device_id=where(group, lo),
            device_id_type=mesh_id,
        )

    sorter = ones_where(
        (block, block),
        lambda r, c: c == (r % tops) * low + (r // tops % groups) * n_lo + r // (tops * groups),
    )
    hop_in[0].wait()
    hop0[...] = dot_nn(sorter, hop[0]).astype(BF16).reshape(hop0.shape)
    for copy in amp_in:
        copy.wait()
    greeted = False
    for side_step in side_steps:
        side = lax.rem(my_side + side_step, SIDES)
        for lo_step in range(n_lo):
            lo = lax.rem(my_lo + lo_step, n_lo)
            for b in range(spans):
                first = dot_nt(hop0[lo, side], amp[b]).astype(BF16)
                packed[lo, pl.ds(side * near, near), b] = first.reshape(near, tops, block)
            if not greeted:
                pl.semaphore_wait(barrier, devices - 1)
                greeted = True
            each(side_step, lo_step, lambda g, l: out_copy(g, l).start(), end=near // 2)
        for lo_step in range(n_lo):
            each(side_step, lo_step, lambda g, l: out_copy(g, l).start(), near // 2)
    own_out = pltpu.make_async_copy(
        packed.at[my_lo, my_group], moved.at[my_lo, my_group], own_sem.at[0]
    )
    own_out.start()

    for copy in hop_in[1:]:
        copy.wait()
    for b in range(spans):
        hop1[b] = (
            hop[1].reshape(groups, spans, tops, block)[:, b].reshape(SIDES, rows, block)
        )
    unzip = ones_where((block, block), lambda r, c: c == (r % halves) * n_lo + r // halves)
    hop2[...] = dot_nn(unzip, hop[2]).T.astype(BF16)
    hop3[...] = hop[3].astype(F32).T.astype(BF16).reshape(hop3.shape)
    at = lax.broadcasted_iota(jnp.int32, (block, 16), 0)
    span, group, top = at // (tops * groups), at // tops % groups, at % tops
    ups = ((group * spans + span) * tops + top) * low + me
    site_r = lax.broadcasted_iota(jnp.int32, (block, 16), 1)
    strength = jnp.zeros((block, 16), F32)
    for i in range(SITES):
        strength = jnp.where(site_r == i, seed_ref[i].astype(F32), strength)
    up_part = (((ups >> site_r) & 1).astype(F32) * strength).astype(BF16)
    downs = lax.broadcasted_iota(jnp.int32, (16, n_lo * block), 1)
    site_c = lax.broadcasted_iota(jnp.int32, (16, n_lo * block), 0)
    down_part = ((downs >> site_c) & 1).astype(F32).astype(BF16)
    for lo in range(n_lo):
        part = dot_nn(up_part, down_part[:, lo * block : (lo + 1) * block])
        factor[lo] = jnp.exp(-COUPLING * part).reshape(factor.shape[1:])
    own_out.wait()

    def two_passes(lo, b, side):
        second = dot_nn(hop1[b, side], moved[lo].reshape(block, block))
        mixed = (second * factor[lo, b, side]).astype(BF16)
        return dot_nn(mixed, hop2[...]).astype(BF16)

    for lo_step in range(n_lo):
        for side_step in side_steps:
            each(side_step, lo_step, lambda g, l: in_copy(g, l).wait_recv())
        lo = lax.rem(my_lo + lo_step, n_lo)
        if lo_step < n_lo - 1:
            for b in range(spans):
                for side in range(SIDES):
                    third[lo_step, b, side] = two_passes(lo, b, side)
    last_lo = lo
    for side_step in side_steps:
        for b in range(spans):
            side = lax.rem(my_side + side_step, SIDES)
            thirds = [third[k, b, side] for k in range(n_lo - 1)]
            thirds.append(two_passes(last_lo, b, side))
            for r in range(n_lo):
                total = sum(
                    dot_nn(
                        thirds[k][:, r * halves : (r + 1) * halves],
                        hop3[lax.rem(my_lo + k, n_lo)],
                    )
                    for k in range(n_lo)
                ).astype(BF16)
                for lo in range(n_lo):
                    piece = total[:, lo * halves : (lo + 1) * halves]
                    fourth[
                        lo, b, pl.ds(side * near, near), :, r * halves : (r + 1) * halves
                    ] = piece.reshape(near, tops, halves)
            for begin in (0, near // 2):
                for lo_step in range(n_lo):
                    each(
                        side_step,
                        lo_step,
                        lambda g, l: back_copy(b, g, l).start(),
                        begin,
                        begin + near // 2,
                    )
    own_back = [
        pltpu.make_async_copy(
            fourth.at[my_lo, b, my_group],
            final.at[b, my_lo * groups + my_group],
            own_sem.at[1 + b],
        )
        for b in range(spans)
    ]
    for copy in own_back:
        copy.start()
    zipper = ones_where((block, block), lambda r, c: r == (c % halves) * n_lo + c // halves)
    for b in range(spans):
        own_back[b].wait()
        for lo_step in range(n_lo):
            for side_step in side_steps:
                each(side_step, lo_step, lambda g, l: home_copy(b, g, l).wait_recv())
        turned = dot_nt(zipper, final[b].reshape(block, block)).astype(BF16)
        out_ref[:, b * block : (b + 1) * block] = dot_nn(turned, sorter).astype(BF16)

    def drain(group, lo):
        out_copy(group, lo).wait_send()
        for b in range(spans):
            back_copy(b, group, lo).wait_send()

    for lo_step in range(n_lo):
        for side_step in side_steps:
            each(side_step, lo_step, drain)


def by_kernel(counts, amplitudes, hop_blocks, coupling_seed):
    n_hi, n_mid, n_lo = counts
    groups, devices = n_hi * n_mid, n_hi * n_mid * n_lo
    block = hop_blocks.shape[1]
    down_rows, up_cols = amplitudes.shape
    low = up_cols * groups // block
    tops = block // low
    spans = up_cols // block
    rows = groups // SIDES * tops
    return pl.pallas_call(
        functools.partial(step_kernel, counts, low),
        out_shape=jax.ShapeDtypeStruct((down_rows, up_cols), BF16),
        in_specs=[
            pl.BlockSpec(memory_space=pltpu.HBM),
            pl.BlockSpec(memory_space=pltpu.HBM),
            pl.BlockSpec(memory_space=pltpu.SMEM),
        ],
        out_specs=pl.BlockSpec(memory_space=pltpu.VMEM),
        scratch_shapes=[
            pltpu.VMEM((spans, block, block), BF16),
            pltpu.VMEM(hop_blocks.shape, BF16),
            pltpu.VMEM((n_lo, SIDES, rows, block), BF16),
            pltpu.VMEM((spans, SIDES, rows, block), BF16),
            pltpu.VMEM((block, block), BF16),
            pltpu.VMEM((n_lo, block // n_lo, block), BF16),
            pltpu.VMEM((n_lo, groups, spans, tops, block), BF16),
            pltpu.VMEM((n_lo, groups, spans, tops, block), BF16),
            pltpu.VMEM((n_lo, spans, SIDES, rows, block), F32),
            pltpu.VMEM((n_lo - 1, spans, SIDES, rows, block), BF16),
            pltpu.VMEM((n_lo, spans, groups, tops, block), BF16),
            pltpu.VMEM((spans, low, tops, block), BF16),
            pltpu.SemaphoreType.DMA((4 + spans,)),
            pltpu.SemaphoreType.DMA((1 + spans,)),
            pltpu.SemaphoreType.DMA((1 + spans, devices)),
            pltpu.SemaphoreType.DMA((1 + spans, devices)),
        ],
        compiler_params=pltpu.CompilerParams(
            collective_id=0, has_side_effects=True, vmem_limit_bytes=60 * 1024 * 1024
        ),
        name="trotter_step",
    )(amplitudes, hop_blocks, coupling_seed)


def on_device(counts, amplitudes, hop_blocks, coupling_seed):
    n_hi, n_mid, n_lo = counts
    groups, devices = n_hi * n_mid, n_hi * n_mid * n_lo
    block = hop_blocks.shape[1]
    down_rows, up_cols = amplitudes.shape
    low = up_cols * groups // block
    fits = (
        low == devices
        and down_rows == block
        and up_cols % block == 0
        and block % (low * 16) == 0
        and n_lo > 1
        and n_hi % SIDES == 0
        and groups & (groups - 1) == 0
        and groups >= 2 * SIDES
        and block % (n_lo * 128) == 0
        and block // groups == (up_cols // block) * (block // low)
    )
    if fits:
        return by_kernel(counts, amplitudes, hop_blocks, coupling_seed)
    return by_collectives(amplitudes, hop_blocks, coupling_seed)


def solution(mesh):
    counts = tuple(mesh.shape[name] for name in AXES)
    in_specs = (P("lo", ("hi", "mid")), P(), P())
    out_specs = P("lo", ("hi", "mid"))
    return jax.shard_map(
        functools.partial(on_device, counts),
        mesh=mesh,
        in_specs=in_specs,
        out_specs=out_specs,
        check_vma=False,
    )
```

```python
import functools

import jax
import jax.numpy as jnp
from jax import lax
from jax.experimental import pallas as pl
from jax.experimental.pallas import tpu as pltpu
from jax.sharding import PartitionSpec as P

SITES = 14
COUPLING = 0.06
AXES = ("hi", "mid", "lo")
SIDES = 2
F32, BF16 = jnp.float32, jnp.bfloat16


def occupancy(indices):
    site_ids = jnp.arange(SITES, dtype=jnp.int32)
    return (indices[:, None] >> site_ids[None, :] & 1).astype(jnp.float32)


def diagonal_factor(up_index, down_index, coupling_seed):
    up_occupied = occupancy(up_index)
    down_occupied = occupancy(down_index)
    strength = COUPLING * coupling_seed.astype(jnp.float32)
    energy = jnp.dot(
        up_occupied * strength[None, :], down_occupied.T, precision=lax.Precision.HIGHEST
    )
    return jnp.exp(-energy)


def by_collectives(amplitudes, hop_blocks, coupling_seed):
    block = hop_blocks.shape[1]
    down_rows, up_cols = amplitudes.shape
    groups = lax.axis_size(("hi", "mid"))
    lo_count = lax.axis_size("lo")
    split_view = amplitudes.reshape(down_rows, up_cols // block, block)
    first_pass = jnp.einsum(
        "dav,wv->awd", split_view, hop_blocks[0], preferred_element_type=jnp.float32
    ).astype(jnp.bfloat16)
    local_top = block // groups
    remainder = up_cols // local_top
    first_pass = first_pass.reshape(local_top, remainder, down_rows)
    moved = lax.all_to_all(first_pass, ("hi", "mid"), split_axis=1, concat_axis=0, tiled=True)
    second_pass = jnp.einsum(
        "gh,hpd->gpd", hop_blocks[1], moved, preferred_element_type=jnp.float32
    )
    span_low = remainder // groups
    up_index = (
        jnp.arange(block, dtype=jnp.int32)[:, None] * remainder
        + lax.axis_index(("hi", "mid")) * span_low
        + jnp.arange(span_low, dtype=jnp.int32)[None, :]
    ).reshape(-1)
    down_index = lax.axis_index("lo") * down_rows + jnp.arange(down_rows, dtype=jnp.int32)
    factor = diagonal_factor(up_index, down_index, coupling_seed).reshape(
        block, span_low, down_rows
    )
    mixed_pass = (second_pass * factor).astype(jnp.bfloat16)
    returned = lax.all_to_all(
        mixed_pass, ("hi", "mid"), split_axis=0, concat_axis=1, tiled=True
    ).reshape(up_cols, down_rows)
    third_pass = jnp.einsum(
        "ud,ed->eu", returned, hop_blocks[2], preferred_element_type=jnp.float32
    ).astype(jnp.bfloat16)
    gathered = lax.all_to_all(
        third_pass.reshape(block // lo_count, lo_count, up_cols),
        "lo",
        split_axis=1,
        concat_axis=0,
        tiled=True,
    )
    fourth_pass = jnp.einsum(
        "gh,hpu->gpu", hop_blocks[3], gathered, preferred_element_type=jnp.float32
    ).astype(jnp.bfloat16)
    result = lax.all_to_all(fourth_pass, "lo", split_axis=0, concat_axis=1, tiled=True).reshape(
        down_rows, up_cols
    )
    return result


def dot_nn(a, b):
    return lax.dot_general(a, b, (((1,), (0,)), ((), ())), preferred_element_type=F32)


def dot_nt(a, b):
    return lax.dot_general(a, b, (((1,), (1,)), ((), ())), preferred_element_type=F32)


def ones_where(shape, condition):
    rows = lax.broadcasted_iota(jnp.int32, shape, 0)
    cols = lax.broadcasted_iota(jnp.int32, shape, 1)
    return jnp.where(condition(rows, cols), 1.0, 0.0).astype(F32).astype(BF16)


def step_kernel(
    counts,
    low,
    amp_hbm,
    hop_hbm,
    seed_ref,
    out_ref,
    amp,
    hop,
    hop0,
    hop1,
    hop2,
    hop3,
    packed,
    moved,
    factor,
    third,
    fourth,
    final,
    in_sem,
    own_sem,
    send_sem,
    recv_sem,
):
    n_hi, n_mid, n_lo = counts
    devices = n_hi * n_mid * n_lo
    groups = n_hi * n_mid
    near = groups // SIDES
    block = hop.shape[1]
    tops = block // low
    spans = amp.shape[0]
    halves = block // n_lo
    rows = near * tops
    my_hi, my_mid, my_lo = (lax.axis_index(name) for name in AXES)
    my_group = my_hi * n_mid + my_mid
    my_side = my_group // near
    me = my_group * n_lo + my_lo
    mesh_id = pl.DeviceIdType.MESH

    hop_in = [
        pltpu.make_async_copy(hop_hbm.at[k], hop.at[k], in_sem.at[k]) for k in range(4)
    ]
    amp_in = [
        pltpu.make_async_copy(
            amp_hbm.at[:, b * block : (b + 1) * block], amp.at[b], in_sem.at[4 + b]
        )
        for b in range(spans)
    ]
    hop_in[0].start()
    for copy in amp_in:
        copy.start()
    for copy in hop_in[1:]:
        copy.start()

    def spot(side_step, lo_step, k):
        side = lax.rem(my_side + side_step, SIDES)
        group = side * near + lax.rem(lax.rem(my_group, near) + 3 * k, near)
        return group, lax.rem(my_lo + lo_step, n_lo)

    def where(group, lo):
        return group // n_mid, lax.rem(group, n_mid), lo

    def each(side_step, lo_step, act):
        def body(k, carry):
            act(*spot(side_step, lo_step, k))
            return carry

        lax.fori_loop(1 if side_step == lo_step == 0 else 0, near, body, 0)

    side_steps = [*range(1, SIDES), 0]
    barrier = pltpu.get_barrier_semaphore()

    def greet(group, lo):
        pl.semaphore_signal(
            barrier, inc=1, device_id=where(group, lo), device_id_type=mesh_id
        )

    for lo_step in range(n_lo):
        for side_step in side_steps:
            each(side_step, lo_step, greet)

    def out_copy(group, lo):
        return pltpu.make_async_remote_copy(
            src_ref=packed.at[lo, group],
            dst_ref=moved.at[my_lo, my_group],
            send_sem=send_sem.at[0, group * n_lo + lo],
            recv_sem=recv_sem.at[0, me],
            device_id=where(group, lo),
            device_id_type=mesh_id,
        )

    def in_copy(group, lo):
        return pltpu.make_async_remote_copy(
            src_ref=packed.at[lo, group],
            dst_ref=moved.at[lo, group],
            send_sem=send_sem.at[0, group * n_lo + lo],
            recv_sem=recv_sem.at[0, group * n_lo + lo],
            device_id=where(group, lo),
            device_id_type=mesh_id,
        )

    def back_copy(b, group, lo):
        return pltpu.make_async_remote_copy(
            src_ref=fourth.at[lo, b, group],
            dst_ref=final.at[b, my_lo * groups + my_group],
            send_sem=send_sem.at[1 + b, group * n_lo + lo],
            recv_sem=recv_sem.at[1 + b, me],
            device_id=where(group, lo),
            device_id_type=mesh_id,
        )

    def home_copy(b, group, lo):
        return pltpu.make_async_remote_copy(
            src_ref=fourth.at[lo, b, group],
            dst_ref=final.at[b, lo * groups + group],
            send_sem=send_sem.at[1 + b, group * n_lo + lo],
            recv_sem=recv_sem.at[1 + b, group * n_lo + lo],
            device_id=where(group, lo),
            device_id_type=mesh_id,
        )

    sorter = ones_where(
        (block, block),
        lambda r, c: c == (r % tops) * low + (r // tops % groups) * n_lo + r // (tops * groups),
    )
    hop_in[0].wait()
    hop0[...] = dot_nn(sorter, hop[0]).astype(BF16).reshape(hop0.shape)
    for copy in amp_in:
        copy.wait()
    greeted = False
    for lo_step in range(n_lo):
        lo = lax.rem(my_lo + lo_step, n_lo)
        for side_step in side_steps:
            side = lax.rem(my_side + side_step, SIDES)
            for b in range(spans):
                first = dot_nt(hop0[lo, side], amp[b]).astype(BF16)
                packed[lo, pl.ds(side * near, near), b] = first.reshape(near, tops, block)
            if not greeted:
                pl.semaphore_wait(barrier, devices - 1)
                greeted = True
            each(side_step, lo_step, lambda g, l: out_copy(g, l).start())
    own_out = pltpu.make_async_copy(
        packed.at[my_lo, my_group], moved.at[my_lo, my_group], own_sem.at[0]
    )
    own_out.start()

    for copy in hop_in[1:]:
        copy.wait()
    for b in range(spans):
        hop1[b] = (
            hop[1].reshape(groups, spans, tops, block)[:, b].reshape(SIDES, rows, block)
        )
    unzip = ones_where((block, block), lambda r, c: c == (r % halves) * n_lo + r // halves)
    hop2[...] = dot_nn(unzip, hop[2]).T.astype(BF16)
    hop3[...] = hop[3].astype(F32).T.astype(BF16).reshape(hop3.shape)
    at = lax.broadcasted_iota(jnp.int32, (block, 16), 0)
    span, group, top = at // (tops * groups), at // tops % groups, at % tops
    ups = ((group * spans + span) * tops + top) * low + me
    site_r = lax.broadcasted_iota(jnp.int32, (block, 16), 1)
    strength = jnp.zeros((block, 16), F32)
    for i in range(SITES):
        strength = jnp.where(site_r == i, seed_ref[i].astype(F32), strength)
    up_part = (((ups >> site_r) & 1).astype(F32) * strength).astype(BF16)
    downs = lax.broadcasted_iota(jnp.int32, (16, n_lo * block), 1)
    site_c = lax.broadcasted_iota(jnp.int32, (16, n_lo * block), 0)
    down_part = ((downs >> site_c) & 1).astype(F32).astype(BF16)
    for lo in range(n_lo):
        part = dot_nn(up_part, down_part[:, lo * block : (lo + 1) * block])
        factor[lo] = jnp.exp(-COUPLING * part).reshape(factor.shape[1:])
    own_out.wait()

    def two_passes(lo, b, side):
        second = dot_nn(hop1[b, side], moved[lo].reshape(block, block))
        mixed = (second * factor[lo, b, side]).astype(BF16)
        return dot_nn(mixed, hop2[...]).astype(BF16)

    for lo_step in range(n_lo):
        for side_step in side_steps:
            each(side_step, lo_step, lambda g, l: in_copy(g, l).wait_recv())
        lo = lax.rem(my_lo + lo_step, n_lo)
        if lo_step < n_lo - 1:
            for b in range(spans):
                for side in range(SIDES):
                    third[lo_step, b, side] = two_passes(lo, b, side)
    last_lo = lo
    for b in range(spans):
        for side_step in side_steps:
            side = lax.rem(my_side + side_step, SIDES)
            thirds = [third[k, b, side] for k in range(n_lo - 1)]
            thirds.append(two_passes(last_lo, b, side))
            for r in range(n_lo):
                total = sum(
                    dot_nn(
                        thirds[k][:, r * halves : (r + 1) * halves],
                        hop3[lax.rem(my_lo + k, n_lo)],
                    )
                    for k in range(n_lo)
                ).astype(BF16)
                for lo in range(n_lo):
                    piece = total[:, lo * halves : (lo + 1) * halves]
                    fourth[
                        lo, b, pl.ds(side * near, near), :, r * halves : (r + 1) * halves
                    ] = piece.reshape(near, tops, halves)
            for lo_step in range(n_lo):
                each(side_step, lo_step, lambda g, l: back_copy(b, g, l).start())
    own_back = [
        pltpu.make_async_copy(
            fourth.at[my_lo, b, my_group],
            final.at[b, my_lo * groups + my_group],
            own_sem.at[1 + b],
        )
        for b in range(spans)
    ]
    for copy in own_back:
        copy.start()
    zipper = ones_where((block, block), lambda r, c: r == (c % halves) * n_lo + c // halves)
    for b in range(spans):
        own_back[b].wait()
        for lo_step in range(n_lo):
            for side_step in side_steps:
                each(side_step, lo_step, lambda g, l: home_copy(b, g, l).wait_recv())
        turned = dot_nt(zipper, final[b].reshape(block, block)).astype(BF16)
        out_ref[:, b * block : (b + 1) * block] = dot_nn(turned, sorter).astype(BF16)

    def drain(group, lo):
        out_copy(group, lo).wait_send()
        for b in range(spans):
            back_copy(b, group, lo).wait_send()

    for lo_step in range(n_lo):
        for side_step in side_steps:
            each(side_step, lo_step, drain)


def by_kernel(counts, amplitudes, hop_blocks, coupling_seed):
    n_hi, n_mid, n_lo = counts
    groups, devices = n_hi * n_mid, n_hi * n_mid * n_lo
    block = hop_blocks.shape[1]
    down_rows, up_cols = amplitudes.shape
    low = up_cols * groups // block
    tops = block // low
    spans = up_cols // block
    rows = groups // SIDES * tops
    return pl.pallas_call(
        functools.partial(step_kernel, counts, low),
        out_shape=jax.ShapeDtypeStruct((down_rows, up_cols), BF16),
        in_specs=[
            pl.BlockSpec(memory_space=pltpu.HBM),
            pl.BlockSpec(memory_space=pltpu.HBM),
            pl.BlockSpec(memory_space=pltpu.SMEM),
        ],
        out_specs=pl.BlockSpec(memory_space=pltpu.VMEM),
        scratch_shapes=[
            pltpu.VMEM((spans, block, block), BF16),
            pltpu.VMEM(hop_blocks.shape, BF16),
            pltpu.VMEM((n_lo, SIDES, rows, block), BF16),
            pltpu.VMEM((spans, SIDES, rows, block), BF16),
            pltpu.VMEM((block, block), BF16),
            pltpu.VMEM((n_lo, block // n_lo, block), BF16),
            pltpu.VMEM((n_lo, groups, spans, tops, block), BF16),
            pltpu.VMEM((n_lo, groups, spans, tops, block), BF16),
            pltpu.VMEM((n_lo, spans, SIDES, rows, block), F32),
            pltpu.VMEM((n_lo - 1, spans, SIDES, rows, block), BF16),
            pltpu.VMEM((n_lo, spans, groups, tops, block), BF16),
            pltpu.VMEM((spans, low, tops, block), BF16),
            pltpu.SemaphoreType.DMA((4 + spans,)),
            pltpu.SemaphoreType.DMA((1 + spans,)),
            pltpu.SemaphoreType.DMA((1 + spans, devices)),
            pltpu.SemaphoreType.DMA((1 + spans, devices)),
        ],
        compiler_params=pltpu.CompilerParams(
            collective_id=0, has_side_effects=True, vmem_limit_bytes=60 * 1024 * 1024
        ),
        name="trotter_step",
    )(amplitudes, hop_blocks, coupling_seed)


def on_device(counts, amplitudes, hop_blocks, coupling_seed):
    n_hi, n_mid, n_lo = counts
    groups, devices = n_hi * n_mid, n_hi * n_mid * n_lo
    block = hop_blocks.shape[1]
    down_rows, up_cols = amplitudes.shape
    low = up_cols * groups // block
    fits = (
        low == devices
        and down_rows == block
        and up_cols % block == 0
        and block % (low * 16) == 0
        and n_lo > 1
        and n_hi % SIDES == 0
        and groups // SIDES % 3 != 0
        and block % (n_lo * 128) == 0
        and block // groups == (up_cols // block) * (block // low)
    )
    if fits:
        return by_kernel(counts, amplitudes, hop_blocks, coupling_seed)
    return by_collectives(amplitudes, hop_blocks, coupling_seed)


def solution(mesh):
    counts = tuple(mesh.shape[name] for name in AXES)
    in_specs = (P("lo", ("hi", "mid")), P(), P())
    out_specs = P("lo", ("hi", "mid"))
    return jax.shard_map(
        functools.partial(on_device, counts),
        mesh=mesh,
        in_specs=in_specs,
        out_specs=out_specs,
        check_vma=False,
    )
```
